32 devices in a mesh: rep: 2 (over y), hid: 8 (over z, x), wid: 2 (over core).
Axes of the slice: x: 2, y: 2, z: 4, core: 2. Of those that a mesh axis runs over, the one named last changes fastest.
Arguments:
- states: float32 [32, 8192], P(('rep', 'hid'), 'wid'), parts along dimension 0, may hold values from -6 to 6
- norm_gain: float32 [8192], P('wid'), may hold values from 0.25 to 1.75
- gate_weight: bfloat16 [8192, 16384], P('wid', 'hid'), may hold values from -0.0625 to 0.0625
- up_weight: bfloat16 [8192, 16384], P('wid', 'hid'), may hold values from -0.0625 to 0.0625
- down_weight: bfloat16 [16384, 8192], P('hid', 'wid'), may hold values from -0.046875 to 0.046875
Outputs:
- updated: float32 [32, 8192], P(('rep', 'hid'), 'wid'), parts along dimension 0
The draws below stay inside these ranges and needn't reach their ends.
There are 2 independent parts, one for each index of `rep`. The reference program is written for one: setup_inputs(seed, part) draws one part's arguments, and reference() takes and returns one part's arrays. A program takes and returns all parts, laid end to end along the dimension named above; an argument that names none is the same for every part. Nothing has to cross between parts.
All inputs are finite; a program needn't handle non-finite values.
Results may differ from the reference program's by a relative error of at most 0.0029.
Values may be sent and summed in bfloat16 or wider, within the bound.
No kernel may reach another device: no remote copies, remote signals or barrier semaphores. Data moves between devices by JAX's collectives and lax.ppermute only.
A program may use at most 128 MiB of HBM per device.

```python
import jax
import jax.numpy as jnp
from jax import lax

D = 8192
FF = 16384
STREAMS = 16


def steps_of(key, extent, shards, least, high):
    def one(position, shards_of):
        draws = jax.random.uniform(jax.random.fold_in(jax.random.fold_in(key, 6), position), (shards_of,), jnp.float32, least / len(shards), high / len(shards))
        return jnp.repeat(jnp.exp(draws), extent[position] // shards_of).reshape((-1,) + (1,) * (len(extent) - position - 1))

    level = one(*shards[0])
    for cut in shards[1:]:
        level = level * one(*cut)
    return level


def centred(stream_key, shape, scale, limit, pieces=(), dtype=jnp.bfloat16):
    gain = steps_of(stream_key, shape, pieces, -0.22, 0.18) if pieces else 1.0
    result = jax.random.normal(stream_key, shape, jnp.float32) * scale * gain
    return jnp.minimum(jnp.maximum(result, -limit), limit).astype(dtype)


def setup_inputs(seed: int = 0, part: int = 0) -> dict:
    splits = jax.random.split(jax.random.key(seed), 6)
    part_keys = jax.random.split(jax.random.fold_in(splits[5], part), 6)
    states = centred(part_keys[0], (STREAMS, D), 1.0, 6.0, ((0, 8), (1, 2)), jnp.float32)
    norm_gain = jnp.clip(1.0 + 0.15 * jax.random.normal(splits[1], (D,), jnp.float32), 0.25, 1.75)
    gate_weight = centred(splits[2], (D, FF), D ** -0.5, 0.0625, ((0, 2), (1, 8)))
    up_weight = centred(splits[3], (D, FF), D ** -0.5, 0.0625, ((0, 2), (1, 8)))
    down_weight = centred(splits[4], (FF, D), FF ** -0.5, 0.046875, ((0, 8), (1, 2)))
    return {"states": states, "norm_gain": norm_gain, "gate_weight": gate_weight, "up_weight": up_weight, "down_weight": down_weight}


def reference(states, norm_gain, gate_weight, up_weight, down_weight):
    power = lax.optimization_barrier(jnp.mean(states * states, axis=1, keepdims=True))
    normed = (states * norm_gain[None, :] * jax.lax.rsqrt(power + 1e-05)).astype(jnp.bfloat16)
    gate = jnp.dot(normed, gate_weight, preferred_element_type=jnp.float32)
    up = jnp.dot(normed, up_weight, preferred_element_type=jnp.float32)
    hidden = (jax.nn.silu(gate) * up).astype(jnp.bfloat16)
    return states + jnp.dot(hidden, down_weight, preferred_element_type=jnp.float32)
```

```python
import jax
import jax.numpy as jnp
from jax import lax
from jax.experimental import pallas as pl
from jax.experimental.pallas import tpu as pltpu
from jax.sharding import PartitionSpec as P

EPS = 1e-05
F32, BF16 = jnp.float32, jnp.bfloat16


def call(kernel, out, *args, name, flops=0, scratch=(), limit=4 << 20):
    spec = pl.BlockSpec(memory_space=pltpu.VMEM)
    return pl.pallas_call(
        kernel,
        out_shape=out,
        in_specs=[spec] * len(args),
        out_specs=spec,
        scratch_shapes=scratch,
        compiler_params=pltpu.CompilerParams(vmem_limit_bytes=limit),
        cost_estimate=pl.CostEstimate(flops=flops, bytes_accessed=0, transcendentals=0),
        name=name,
    )(*args)


def dot(a, b):
    return jnp.dot(a, b, preferred_element_type=F32)


def prepare_kernel(states_ref, others_ref, gain_ref, out_ref):
    states, others = states_ref[...], others_ref[...]
    squares = jnp.sum(states * states, axis=1, keepdims=True)
    squares += jnp.sum(others * others, axis=1, keepdims=True)
    scale = lax.rsqrt(squares / (2 * states.shape[1]) + EPS)
    normed = (states * gain_ref[...] * scale).astype(BF16)
    for k in range(out_ref.shape[0]):
        out_ref[k] = normed


def project_kernel(gathered_ref, weight_ref, out_ref):
    x = gathered_ref[...].reshape(out_ref.shape[0], weight_ref.shape[0])
    out_ref[...] = dot(x, weight_ref[...])


def down_kernel(gate_ref, gate_other_ref, up_ref, up_other_ref, down_ref, out_ref):
    gate = gate_ref[...] + gate_other_ref[...]
    up = up_ref[...] + up_other_ref[...]
    hidden = (gate / (1 + jnp.exp(-gate)) * up).astype(BF16)
    out_ref[...] = dot(hidden, down_ref[...]).astype(BF16).reshape(out_ref.shape)


def finish_kernel(states_ref, parts_ref, out_ref):
    total = states_ref[...]
    for k in range(parts_ref.shape[0]):
        total += parts_ref[k].astype(F32)
    out_ref[...] = total


def solution(mesh):
    hid = mesh.shape["hid"]

    def local(states, norm_gain, gate_weight, up_weight, down_weight):
        rows, half = states.shape
        width = gate_weight.shape[1]
        streams = rows * hid
        struct = jax.ShapeDtypeStruct

        def swap(value):
            return lax.ppermute(value, "wid", [(0, 1), (1, 0)])

        normed = call(
            prepare_kernel,
            struct((hid, rows, half), BF16),
            states,
            swap(states),
            norm_gain[None, :],
            name="prepare",
            flops=100_000_000_000,
            limit=1 << 20,
        )
        gathered = lax.all_to_all(normed, "hid", 0, 0)
        part = struct((streams, width), F32)
        gate = call(project_kernel, part, gathered, gate_weight, name="gate")
        up = call(project_kernel, part, gathered, up_weight, name="up")
        mixed = call(
            down_kernel,
            struct((hid, rows, half), BF16),
            gate,
            swap(gate),
            up,
            swap(up),
            down_weight,
            name="down",
        )
        parts = lax.all_to_all(mixed, "hid", 0, 0)
        return call(finish_kernel, struct((rows, half), F32), states, parts, name="finish")

    return jax.shard_map(
        local,
        mesh=mesh,
        in_specs=(
            P(("rep", "hid"), "wid"),
            P("wid"),
            P("wid", "hid"),
            P("wid", "hid"),
            P("hid", "wid"),
        ),
        out_specs=P(("rep", "hid"), "wid"),
        check_vma=False,
    )
```

```python
import jax
import jax.numpy as jnp
from jax import lax
from jax.experimental import pallas as pl
from jax.experimental.pallas import tpu as pltpu
from jax.sharding import PartitionSpec as P

EPS = 1e-05
F32, BF16 = jnp.float32, jnp.bfloat16
VMEM, HBM = pltpu.MemorySpace.VMEM, pltpu.MemorySpace.HBM


def call(kernel, out, *args, name, flops=0, space=VMEM, scratch=(), limit=4 << 20):
    return pl.pallas_call(
        kernel,
        out_shape=out,
        in_specs=[pl.BlockSpec(memory_space=space)] * len(args),
        out_specs=jax.tree.map(lambda _: pl.BlockSpec(memory_space=VMEM), out),
        scratch_shapes=scratch,
        compiler_params=pltpu.CompilerParams(vmem_limit_bytes=limit),
        cost_estimate=pl.CostEstimate(flops=flops, bytes_accessed=0, transcendentals=0),
        name=name,
    )(*args)


def dot(a, b):
    return jnp.dot(a, b, preferred_element_type=F32)


def load_kernel(states_hbm, gain_hbm, scaled_ref, squares_ref, states_ref, gain_ref, sems):
    copies = [
        pltpu.make_async_copy(states_hbm, states_ref, sems.at[0]),
        pltpu.make_async_copy(gain_hbm, gain_ref, sems.at[1]),
    ]
    for copy in copies:
        copy.start()
    for copy in copies:
        copy.wait()
    states = states_ref[...]
    scaled_ref[...] = states * gain_ref[...]
    squares_ref[...] = jnp.sum(states * states, axis=1, keepdims=True)


def prepare_kernel(scaled_ref, squares_ref, others_ref, out_ref):
    others = others_ref[...]
    squares = squares_ref[...] + jnp.sum(others * others, axis=1, keepdims=True)
    scale = lax.rsqrt(squares / (2 * others.shape[1]) + EPS)
    normed = (scaled_ref[...] * scale).astype(BF16)
    for k in range(out_ref.shape[0]):
        out_ref[k] = normed


def first_kernel(gathered_ref, gate_ref, up_ref, out_ref):
    streams, total = out_ref.shape
    width = gate_ref.shape[1]
    x = gathered_ref[...].reshape(streams, gate_ref.shape[0])
    out_ref[:, :width] = dot(x, gate_ref[...])
    out_ref[:, width:] = dot(x, up_ref[:, : total - width])


def second_kernel(gathered_ref, up_ref, *refs):
    out_ref = refs[-1]
    streams, count = out_ref.shape
    x = gathered_ref[...].reshape(streams, up_ref.shape[0])
    out_ref[...] = dot(x, up_ref[:, up_ref.shape[1] - count :])


def activate(gate, up):
    return (gate / (1 + jnp.exp(-gate)) * up).astype(BF16)


def down_kernel(first_ref, first_other_ref, down_ref, out_ref):
    width = down_ref.shape[0]
    count = first_ref.shape[1] - width
    gate = first_ref[:, :count] + first_other_ref[:, :count]
    up = first_ref[:, width:] + first_other_ref[:, width:]
    out = dot(activate(gate, up), down_ref[:count, :])
    out_ref[...] = out.astype(out_ref.dtype).reshape(out_ref.shape)


def add_kernel(first_ref, first_other_ref, second_ref, second_other_ref, down_ref, sum_ref, out_ref):
    width = down_ref.shape[0]
    count = first_ref.shape[1] - width
    gate = first_ref[:, count:width] + first_other_ref[:, count:width]
    up = second_ref[...] + second_other_ref[...]
    out = sum_ref[...] + dot(activate(gate, up), down_ref[count:, :])
    out_ref[...] = out.astype(out_ref.dtype).reshape(out_ref.shape)


def finish_kernel(states_ref, parts_ref, out_ref):
    total = states_ref[...]
    for k in range(parts_ref.shape[0]):
        total += parts_ref[k].astype(F32)
    out_ref[...] = total


def solution(mesh):
    hid = mesh.shape["hid"]

    def local(states, norm_gain, gate_weight, up_weight, down_weight):
        rows, half = states.shape
        width = gate_weight.shape[1]
        streams = rows * hid
        count = width // 2 if width % 256 == 0 else width
        struct = jax.ShapeDtypeStruct

        def swap(value):
            return lax.ppermute(value, "wid", [(0, 1), (1, 0)])

        scaled, squares = call(
            load_kernel,
            (struct((rows, half), F32), struct((rows, 1), F32)),
            pltpu.with_memory_space_constraint(states, HBM),
            pltpu.with_memory_space_constraint(norm_gain[None, :], HBM),
            name="load",
            flops=100_000_000_000,
            space=pl.ANY,
            limit=1 << 20,
            scratch=[
                pltpu.VMEM((rows, half), F32),
                pltpu.VMEM((1, half), F32),
                pltpu.SemaphoreType.DMA((2,)),
            ],
        )
        normed = call(
            prepare_kernel,
            struct((hid, rows, half), BF16),
            scaled,
            squares,
            swap(states),
            name="prepare",
            limit=1 << 20,
        )
        gathered = lax.all_to_all(normed, "hid", 0, 0)

        first = call(
            first_kernel,
            struct((streams, width + count), F32),
            gathered,
            gate_weight,
            up_weight,
            name="first",
            limit=17 << 18,
        )
        first_other = swap(first)
        out = struct((hid, rows, half), BF16)
        if count == width:
            mixed = call(down_kernel, out, first, first_other, down_weight, name="down")
        else:
            second = call(
                second_kernel,
                struct((streams, width - count), F32),
                gathered,
                up_weight,
                name="second",
                limit=4 << 20,
            )
            second_other = swap(second)
            mixed = call(
                down_kernel,
                struct((streams, half), F32),
                first,
                first_other,
                down_weight,
                name="down",
                limit=3 << 20,
            )
            mixed = call(
                add_kernel,
                out,
                first,
                first_other,
                second,
                second_other,
                down_weight,
                mixed,
                name="add",
                limit=3 << 20,
            )
        summands = lax.all_to_all(mixed, "hid", 0, 0)
        return call(finish_kernel, struct((rows, half), F32), states, summands, name="finish")

    return jax.shard_map(
        local,
        mesh=mesh,
        in_specs=(
            P(("rep", "hid"), "wid"),
            P("wid"),
            P("wid", "hid"),
            P("wid", "hid"),
            P("hid", "wid"),
        ),
        out_specs=P(("rep", "hid"), "wid"),
        check_vma=False,
    )
```

```python
import functools

import jax
import jax.numpy as jnp
from jax import lax
from jax.experimental import pallas as pl
from jax.experimental.pallas import tpu as pltpu
from jax.sharding import PartitionSpec as P

EPS = 1e-05
F32, BF16 = jnp.float32, jnp.bfloat16
VMEM, HBM = pltpu.MemorySpace.VMEM, pltpu.MemorySpace.HBM


def call(kernel, out, *args, name, flops=0, space=VMEM, scratch=(), limit=4 << 20):
    return pl.pallas_call(
        kernel,
        out_shape=out,
        in_specs=[pl.BlockSpec(memory_space=space)] * len(args),
        out_specs=jax.tree.map(lambda _: pl.BlockSpec(memory_space=VMEM), out),
        scratch_shapes=scratch,
        compiler_params=pltpu.CompilerParams(vmem_limit_bytes=limit),
        cost_estimate=pl.CostEstimate(flops=flops, bytes_accessed=0, transcendentals=0),
        name=name,
    )(*args)


def dot(a, b):
    return jnp.dot(a, b, preferred_element_type=F32)


def load_kernel(states_hbm, gain_hbm, scaled_ref, squares_ref, states_ref, gain_ref, sems):
    copies = [
        pltpu.make_async_copy(states_hbm, states_ref, sems.at[0]),
        pltpu.make_async_copy(gain_hbm, gain_ref, sems.at[1]),
    ]
    for copy in copies:
        copy.start()
    for copy in copies:
        copy.wait()
    states = states_ref[...]
    scaled_ref[...] = states * gain_ref[...]
    squares_ref[...] = jnp.sum(states * states, axis=1, keepdims=True)


def prepare_kernel(scaled_ref, squares_ref, others_ref, out_ref):
    others = others_ref[...]
    squares = squares_ref[...] + jnp.sum(others * others, axis=1, keepdims=True)
    scale = lax.rsqrt(squares / (2 * others.shape[1]) + EPS)
    normed = (scaled_ref[...] * scale).astype(BF16)
    for k in range(out_ref.shape[0]):
        out_ref[k] = normed


def project_kernel(gathered_ref, gate_ref, up_ref, *out_refs):
    streams, double = out_refs[0].shape
    count = double // 2
    x = gathered_ref[...].reshape(streams, gate_ref.shape[0])
    for side, weight_ref in enumerate((gate_ref, up_ref)):
        product = dot(x, weight_ref[...])
        for k, out_ref in enumerate(out_refs):
            out_ref[:, side * count : (side + 1) * count] = product[:, k * count : (k + 1) * count]


def down_kernel(start, mine_ref, other_ref, down_ref, *refs):
    count = mine_ref.shape[1] // 2
    total = mine_ref[...] + other_ref[...]
    gate, up = total[:, :count], total[:, count:]
    hidden = (gate / (1 + jnp.exp(-gate)) * up).astype(BF16)
    product = dot(hidden, down_ref[start : start + count, :])
    if len(refs) == 2:
        product += refs[0][...]
    out_ref = refs[-1]
    out_ref[...] = product.astype(out_ref.dtype).reshape(out_ref.shape)


def finish_kernel(states_ref, parts_ref, out_ref):
    total = states_ref[...]
    for k in range(parts_ref.shape[0]):
        total += parts_ref[k].astype(F32)
    out_ref[...] = total


def solution(mesh):
    hid = mesh.shape["hid"]

    def local(states, norm_gain, gate_weight, up_weight, down_weight):
        rows, half = states.shape
        width = gate_weight.shape[1]
        streams = rows * hid
        count = width // 2 if width % 256 == 0 else width
        struct = jax.ShapeDtypeStruct

        def swap(value):
            return lax.ppermute(value, "wid", [(0, 1), (1, 0)])

        scaled, squares = call(
            load_kernel,
            (struct((rows, half), F32), struct((rows, 1), F32)),
            pltpu.with_memory_space_constraint(states, HBM),
            pltpu.with_memory_space_constraint(norm_gain[None, :], HBM),
            name="load",
            flops=100_000_000_000,
            space=pl.ANY,
            limit=1 << 20,
            scratch=[
                pltpu.VMEM((rows, half), F32),
                pltpu.VMEM((1, half), F32),
                pltpu.SemaphoreType.DMA((2,)),
            ],
        )
        normed = call(
            prepare_kernel,
            struct((hid, rows, half), BF16),
            scaled,
            squares,
            swap(states),
            name="prepare",
            limit=1 << 20,
        )
        gathered = lax.all_to_all(normed, "hid", 0, 0)

        pieces = width // count
        part = struct((streams, 2 * count), F32)
        parts = call(
            project_kernel,
            (part,) * pieces,
            gathered,
            gate_weight,
            up_weight,
            name="project",
            limit=17 << 18,
        )
        others = [swap(value) for value in parts]
        mixed = ()
        for k in range(pieces):
            last = k == pieces - 1
            mixed = (
                call(
                    functools.partial(down_kernel, k * count),
                    struct((hid, rows, half), BF16) if last else struct((streams, half), F32),
                    parts[k],
                    others[k],
                    down_weight,
                    *mixed,
                    name=f"down{k}",
                    limit=3 << 20,
                ),
            )
        summands = lax.all_to_all(*mixed, "hid", 0, 0)
        return call(finish_kernel, struct((rows, half), F32), states, summands, name="finish")

    return jax.shard_map(
        local,
        mesh=mesh,
        in_specs=(
            P(("rep", "hid"), "wid"),
            P("wid"),
            P("wid", "hid"),
            P("wid", "hid"),
            P("hid", "wid"),
        ),
        out_specs=P(("rep", "hid"), "wid"),
        check_vma=False,
    )
```

```python
import functools

import jax
import jax.numpy as jnp
from jax import lax
from jax.experimental import pallas as pl
from jax.experimental.pallas import tpu as pltpu
from jax.sharding import PartitionSpec as P

EPS = 1e-05
F32, BF16 = jnp.float32, jnp.bfloat16
VMEM, HBM = pltpu.MemorySpace.VMEM, pltpu.MemorySpace.HBM


def call(kernel, out, *args, name, flops=0, space=VMEM, scratch=(), limit=4 << 20):
    return pl.pallas_call(
        kernel,
        out_shape=out,
        in_specs=[pl.BlockSpec(memory_space=space)] * len(args),
        out_specs=jax.tree.map(lambda _: pl.BlockSpec(memory_space=VMEM), out),
        scratch_shapes=scratch,
        compiler_params=pltpu.CompilerParams(vmem_limit_bytes=limit),
        cost_estimate=pl.CostEstimate(flops=flops, bytes_accessed=0, transcendentals=0),
        name=name,
    )(*args)


def dot(a, b):
    return jnp.dot(a, b, preferred_element_type=F32)


def load_kernel(states_hbm, gain_hbm, scaled_ref, squares_ref, states_ref, gain_ref, sems):
    copies = [
        pltpu.make_async_copy(states_hbm, states_ref, sems.at[0]),
        pltpu.make_async_copy(gain_hbm, gain_ref, sems.at[1]),
    ]
    for copy in copies:
        copy.start()
    for copy in copies:
        copy.wait()
    states = states_ref[...]
    scaled_ref[...] = states * gain_ref[...]
    squares_ref[...] = jnp.sum(states * states, axis=1, keepdims=True)


def prepare_kernel(scaled_ref, squares_ref, others_ref, out_ref):
    others = others_ref[...]
    squares = squares_ref[...] + jnp.sum(others * others, axis=1, keepdims=True)
    scale = lax.rsqrt(squares / (2 * others.shape[1]) + EPS)
    normed = (scaled_ref[...] * scale).astype(BF16)
    for k in range(out_ref.shape[0]):
        out_ref[k] = normed


def project_kernel(gathered_ref, gate_ref, up_ref, *out_refs):
    x = gathered_ref[...].reshape(out_refs[0].shape[0], gate_ref.shape[0])
    for side, weight_ref in enumerate((gate_ref, up_ref)):
        product = dot(x, weight_ref[...])
        start = 0
        for out_ref in out_refs:
            count = out_ref.shape[1] // 2
            out_ref[:, side * count : (side + 1) * count] = product[:, start : start + count]
            start += count


def down_kernel(start, mine_ref, other_ref, down_ref, *refs):
    count = mine_ref.shape[1] // 2
    total = mine_ref[...] + other_ref[...]
    gate, up = total[:, :count], total[:, count:]
    hidden = (gate / (1 + jnp.exp(-gate)) * up).astype(BF16)
    product = dot(hidden, down_ref[start : start + count, :])
    if len(refs) == 2:
        product += refs[0][...]
    out_ref = refs[-1]
    out_ref[...] = product.astype(out_ref.dtype).reshape(out_ref.shape)


def finish_kernel(states_ref, parts_ref, out_ref):
    total = states_ref[...]
    for k in range(parts_ref.shape[0]):
        total += parts_ref[k].astype(F32)
    out_ref[...] = total


def solution(mesh):
    hid = mesh.shape["hid"]

    def local(states, norm_gain, gate_weight, up_weight, down_weight):
        rows, half = states.shape
        width = gate_weight.shape[1]
        streams = rows * hid
        counts = (width // 4, width - width // 4) if width % 512 == 0 else (width,)
        struct = jax.ShapeDtypeStruct

        def swap(value):
            return lax.ppermute(value, "wid", [(0, 1), (1, 0)])

        scaled, squares = call(
            load_kernel,
            (struct((rows, half), F32), struct((rows, 1), F32)),
            pltpu.with_memory_space_constraint(states, HBM),
            pltpu.with_memory_space_constraint(norm_gain[None, :], HBM),
            name="load",
            flops=100_000_000_000,
            space=pl.ANY,
            limit=1 << 20,
            scratch=[
                pltpu.VMEM((rows, half), F32),
                pltpu.VMEM((1, half), F32),
                pltpu.SemaphoreType.DMA((2,)),
            ],
        )
        normed = call(
            prepare_kernel,
            struct((hid, rows, half), BF16),
            scaled,
            squares,
            swap(states),
            name="prepare",
            limit=1 << 20,
        )
        gathered = lax.all_to_all(normed, "hid", 0, 0)

        pieces = len(counts)
        parts = call(
            project_kernel,
            tuple(struct((streams, 2 * count), F32) for count in counts),
            gathered,
            gate_weight,
            up_weight,
            name="project",
            limit=17 << 18,
        )
        others = [swap(value) for value in parts]
        mixed = ()
        for k in range(pieces):
            last = k == pieces - 1
            mixed = (
                call(
                    functools.partial(down_kernel, sum(counts[:k])),
                    struct((hid, rows, half), BF16) if last else struct((streams, half), F32),
                    parts[k],
                    others[k],
                    down_weight,
                    *mixed,
                    name=f"down{k}",
                    limit=3 << 20,
                ),
            )
        summands = lax.all_to_all(*mixed, "hid", 0, 0)
        return call(finish_kernel, struct((rows, half), F32), states, summands, name="finish")

    return jax.shard_map(
        local,
        mesh=mesh,
        in_specs=(
            P(("rep", "hid"), "wid"),
            P("wid"),
            P("wid", "hid"),
            P("wid", "hid"),
            P("hid", "wid"),
        ),
        out_specs=P(("rep", "hid"), "wid"),
        check_vma=False,
    )
```
